32 devices in a mesh: dp: 16 (over z, x, core), mp: 2 (over y).
Axes of the slice: x: 2, y: 2, z: 4, core: 2. Of those that a mesh axis runs over, the one named last changes fastest.
Arguments:
- inputs: bfloat16 [8192, 3968], P('dp', 'mp'), may hold values from -6 to 6
- grad_out: bfloat16 [8192, 2048], P('dp', 'mp'), may hold values from -0.25 to 0.25
- error: bfloat16 [32768, 3968], P(('dp', 'mp')), may hold values from -6 to 6
- q_prev: float32 [3968, 64], P('mp'), may hold values from -0.09375 to 0.09375
Outputs:
- new_error: bfloat16 [32768, 3968], P(('dp', 'mp'))
- p_basis: float32 [2048, 64], P('mp')
- q_factor: float32 [3968, 64], P('mp')
The draws below stay inside these ranges and needn't reach their ends.
All inputs are finite; a program needn't handle non-finite values.
Results may differ from the reference program's by a relative error of at most 0.0065.
Values may be sent and summed in bfloat16 or wider, within the bound.
A program may use at most 64 MiB of HBM per device.

```python
import jax
import jax.numpy as jnp
from jax import lax

D = 3968
OUT = 2048
R = 64
TOK_DEV = 512
TOKENS = 8192
ROWS = 32768
N_DP = 16


def block_scale(stream_key, dims, cuts, smallest, top_value):
    level, own = 1.0, jax.random.fold_in(stream_key, 6)
    for dim, parts in cuts:
        steps = jnp.exp(jax.random.uniform(jax.random.fold_in(own, dim), (parts,), jnp.float32, smallest / len(cuts), top_value / len(cuts)))
        level = level * jnp.repeat(steps, dims[dim] // parts).reshape([-1 if axis == dim else 1 for axis in range(len(dims))])
    return level


def noise(rng, shape, scale, limit, split=(), kind=jnp.bfloat16):
    array = jax.random.normal(rng, shape, jnp.float32) * scale
    if len(split) > 0:
        array = block_scale(rng, shape, split, -0.22, 0.18) * array
    return jnp.clip(array, min=-limit, max=limit).astype(kind)


def setup_inputs(seed: int = 0) -> dict:
    arg_keys = jax.random.split(jax.random.key(seed), 5)
    return {
        "inputs": noise(arg_keys[0], (TOKENS, D), 1.0, 6.0, ((0, 16), (1, 2))),
        "grad_out": noise(arg_keys[1], (TOKENS, OUT), TOK_DEV ** -0.5, 0.25, ((0, 16), (1, 2))),
        "error": noise(arg_keys[2], (ROWS, D), 1.0, 6.0, ((0, 32),)),
        "q_prev": noise(arg_keys[3], (D, R), D ** -0.5, 0.09375, ((0, 2),), jnp.float32),
    }


def reference(inputs, grad_out, error, q_prev):
    highest = lax.Precision.HIGHEST
    xs = inputs.reshape(N_DP, TOK_DEV, D)
    gs = grad_out.reshape(N_DP, TOK_DEV, OUT)
    es = error.reshape(N_DP, OUT, D)

    def merged(index):
        xrow = lax.dynamic_index_in_dim(xs, index, 0, False)
        grow = lax.dynamic_index_in_dim(gs, index, 0, False)
        erow = lax.dynamic_index_in_dim(es, index, 0, False)
        prod = lax.dot_general(grow.astype(jnp.float32), xrow.astype(jnp.float32), (((0,), (0,)), ((), ())), preferred_element_type=jnp.float32)
        return prod + erow.astype(jnp.float32)

    def add_p(carry, index):
        return (carry + jnp.dot(merged(index), q_prev, precision=highest), None)
    indices = jnp.arange(N_DP, dtype=jnp.int32)
    psum_all, _ = lax.scan(add_p, jnp.zeros((OUT, R), jnp.float32), indices)
    factor = psum_all / N_DP
    gram = jnp.dot(factor.T, factor, precision=highest)
    ridge = 0.01 * jnp.trace(gram) / R + 1e-06
    gram = gram + ridge * jnp.eye(R, dtype=jnp.float32)
    lower = jnp.linalg.cholesky(gram)
    p_hat = jax.scipy.linalg.solve_triangular(lower, factor.T, lower=True).T

    def add_q(carry, index):
        term = lax.dot_general(merged(index), p_hat, (((0,), (0,)), ((), ())), precision=highest)
        return (carry + term, None)
    qsum_all, _ = lax.scan(add_q, jnp.zeros((D, R), jnp.float32), indices)
    q_factor = qsum_all / N_DP
    approx = jnp.dot(p_hat, q_factor.T, precision=highest)

    def residue(index):
        return (merged(index) - approx).astype(jnp.bfloat16)
    new_error = lax.map(residue, indices).reshape(N_DP * OUT, D)
    return (new_error, p_hat * jnp.sqrt(jnp.float32(OUT)), q_factor)
```

```python
import functools

import jax
import jax.numpy as jnp
from jax import lax
from jax.experimental import pallas as pl
from jax.experimental.pallas import tpu as pltpu
from jax.sharding import PartitionSpec as P

MESH = pl.DeviceIdType.MESH
PIECES = 16
EARLY = 8
TN = (((0,), (0,)), ((), ()))
NT = (((1,), (1,)), ((), ()))


def left_half(shape):
    return lax.broadcasted_iota(jnp.int32, shape, 1) < shape[1] // 2


def fold(value):
    return value + pltpu.roll(value, value.shape[1] // 2, 1)


def split(twice):
    head = twice.astype(jnp.bfloat16)
    rest = (twice - head.astype(jnp.float32)).astype(jnp.bfloat16)
    return jnp.where(left_half(twice.shape), head.astype(jnp.float32), rest.astype(jnp.float32)).astype(jnp.bfloat16)


def pack(twice):
    rows = twice.shape[0] // 2
    return jnp.where(left_half((rows, twice.shape[1])), twice[:rows], twice[rows:])


def unpack(packed):
    other = pltpu.roll(packed, packed.shape[1] // 2, 1)
    left = left_half(packed.shape)
    return jnp.concatenate([jnp.where(left, packed, other), jnp.where(left, other, packed)], axis=0)


def dot(a, b, dims=(((1,), (0,)), ((), ()))):
    return lax.dot_general(a, b, dims, preferred_element_type=jnp.float32)


def inverse_factor(gram, rank):
    shape = (rank, 2 * rank)
    row = lax.broadcasted_iota(jnp.int32, shape, 0)
    col = lax.broadcasted_iota(jnp.int32, shape, 1)
    left = col < rank
    diag = row == col
    trace = jnp.sum(jnp.where(diag, gram, 0.0), keepdims=True)
    ridge = 0.01 * trace / rank + 1e-06
    work = jnp.where(left, gram + jnp.where(diag, ridge, 0.0), jnp.where(col == row + rank, 1.0, 0.0))
    row1 = lax.broadcasted_iota(jnp.int32, (rank, 1), 0)
    for k in range(rank - 1):
        pivot_row = work[k : k + 1, :]
        scaled = pivot_row / pivot_row[:, k : k + 1]
        factor = jnp.where(row1 > k, work[:, k : k + 1], 0.0)
        work = work - factor * scaled
    pivots = jnp.sum(jnp.where(diag, work, 0.0), axis=1, keepdims=True)
    return work * lax.rsqrt(pivots)


def exchange_kernel(
    n_dp, x_ref, g_ref, e_hbm, qd_ref,
    basis_ref, qown_ref, pa_ref, pb_ref, qg_ref, xo_ref,
    e_ref, qs, u_send, u_recv, pw, p1, p2, p3, pg, gs, gr, qf, qw, q1, qb, q2, qc, q3,
    load_sem, x_ssem, x_rsem, ssem, rsem,
):
    dp, mp = lax.axis_index("dp"), lax.axis_index("mp")
    core, xx, zz = lax.rem(dp, 2), lax.rem(dp // 2, 2), dp // 4
    n_z = n_dp // 4
    rank = basis_ref.shape[1]

    def device(d_core, d_x, d_y, k):
        z = lax.rem(zz + k, n_z)
        c = 1 - core if d_core else core
        x = 1 - xx if d_x else xx
        return ((z * 2 + x) * 2 + c, 1 - mp if d_y else mp)

    core_mate, x_mate, y_mate, far_mate = device(1, 0, 0, 0), device(0, 1, 0, 0), device(0, 0, 1, 0), device(0, 1, 1, 0)
    lane = [device(0, 0, 0, k) for k in range(1, n_z)]

    load = pltpu.make_async_copy(e_hbm, e_ref, load_sem)
    load.start()
    barrier = pltpu.get_barrier_semaphore()
    mates = [core_mate, x_mate, y_mate, far_mate] + lane
    for mate in mates:
        pl.semaphore_signal(barrier, inc=1, device_id=mate, device_id_type=MESH)

    used = [0]

    def send(src, dst, mate):
        index = used[0]
        used[0] += 1
        copy = pltpu.make_async_remote_copy(
            src_ref=src, dst_ref=dst, send_sem=ssem.at[index], recv_sem=rsem.at[index],
            device_id=mate, device_id_type=MESH,
        )
        copy.start()
        return copy

    x_rows = x_ref.shape[0] // PIECES

    def x_piece(j):
        part = pl.ds(j * x_rows, x_rows)
        return pltpu.make_async_remote_copy(
            src_ref=x_ref.at[part], dst_ref=xo_ref.at[part], send_sem=x_ssem.at[j], recv_sem=x_rsem.at[j],
            device_id=y_mate, device_id_type=MESH,
        )

    x_copies = [x_piece(j) for j in range(PIECES)]

    qs[mp] = split(qd_ref[...])
    u_own = pack(fold(dot(x_ref[...], qs[mp])))
    u_send[...] = u_own
    pl.semaphore_wait(barrier, len(mates))
    half = qs.shape[1] // 2
    my_half = pl.ds(pl.multiple_of(core * half, 16), half)
    q_copy = send(qs.at[mp, my_half], qs.at[mp, my_half], y_mate)
    u_copy = send(u_send, u_recv, y_mate)
    q_copy.wait()
    q_pass = send(qs.at[1 - mp, my_half], qs.at[1 - mp, my_half], core_mate)
    x_copies[0].start()
    load.wait()
    u_copy.wait()
    u = split(unpack(u_own + u_recv[...]))
    p_part = dot(g_ref[...], u, TN)
    q_pass.wait()
    x_copies[1].start()
    q_all = jnp.concatenate([qs[0], qs[1]], axis=0)
    pw[...] = pack(fold(p_part + dot(e_ref[...], q_all)))

    n = pw.shape[0]
    n1, n2 = n // 2, n // 4
    n3 = n2 // n_z

    def rows(offset, size):
        return pl.ds(pl.multiple_of(offset, size), size)

    b1 = core * n1
    b2 = b1 + xx * n2
    b3 = b2 + zz * n3
    copy = send(pw.at[rows((1 - core) * n1, n1)], p1, core_mate)
    copy.wait()
    pw[rows(b1, n1)] = pw[rows(b1, n1)] + p1[...]
    copy = send(pw.at[rows(b1 + (1 - xx) * n2, n2)], p2, x_mate)
    x_copies[2].start()
    copy.wait()
    pw[rows(b2, n2)] = pw[rows(b2, n2)] + p2[...]
    copies = [
        send(pw.at[rows(b2 + lax.rem(zz + k, n_z) * n3, n3)], p3.at[k - 1], lane[k - 1]) for k in range(1, n_z)
    ]
    x_copies[3].start()
    total = pw[rows(b3, n3)]
    for k, copy in enumerate(copies):
        copy.wait()
        total = total + p3[k]
    pg[rows(b3, n3)] = total * (1.0 / n_dp)
    copies = [send(pg.at[rows(b3, n3)], pg.at[rows(b3, n3)], mate) for mate in lane]
    x_copies[4].start()
    for copy in copies:
        copy.wait()
    copy = send(pg.at[rows(b2, n2)], pg.at[rows(b2, n2)], x_mate)
    x_copies[5].start()
    copy.wait()
    copy = send(pg.at[rows(b1, n1)], pg.at[rows(b1, n1)], core_mate)
    for j in range(6, EARLY):
        x_copies[j].start()
    copy.wait()

    packed = pg[...]
    square = lax.dot_general(packed, packed, TN, precision=lax.Precision.HIGHEST, preferred_element_type=jnp.float32)
    square = square[:rank] + pltpu.roll(square, rank, 1)[rank:]
    gs[...] = square
    copy = send(gs, gr, y_mate)
    for j in range(EARLY, PIECES):
        x_copies[j].start()
    copy.wait()
    inverse = inverse_factor(square + gr[...], rank)
    inverse = jnp.where(left_half(inverse.shape), 0.0, inverse)
    inverse = jnp.concatenate([fold(inverse)] * 2, axis=0)
    shape = inverse.shape
    upper = lax.broadcasted_iota(jnp.int32, shape, 0) < rank
    block = jnp.where(upper == left_half(shape), inverse, 0.0)
    p_hat = unpack(
        lax.dot_general(packed, block, NT, precision=lax.Precision.HIGHEST, preferred_element_type=jnp.float32)
    )
    basis_ref[...] = (p_hat * jnp.sqrt(jnp.float32(2 * n * lax.axis_size("mp"))))[:, :rank]
    head = p_hat.astype(jnp.bfloat16).astype(jnp.float32)
    left = left_half(p_hat.shape)
    width = 2 * rank
    for part, value in enumerate((head, p_hat - head)):
        pa_ref[:, part * width : (part + 1) * width] = jnp.where(left, value, 0.0).astype(jnp.bfloat16)
        pb_ref[:, part * width : (part + 1) * width] = jnp.where(left, 0.0, value).astype(jnp.bfloat16)
    p_pair = split(p_hat)
    v = split(fold(dot(g_ref[...], p_pair)))

    features = e_ref.shape[1]
    qf[pl.ds(features, qf.shape[0] - features)] = jnp.zeros((qf.shape[0] - features, width), jnp.float32)

    @pl.loop(0, features // 128)
    def _(c):
        at = pl.ds(pl.multiple_of(c * 128, 128), 128)
        qf[at] = fold(dot(e_ref[:, at], p_pair, TN))

    own = x_ref.shape[1]
    mine = pl.ds(pl.multiple_of(mp * own, 8), own)
    theirs = pl.ds(pl.multiple_of((1 - mp) * own, 8), own)
    qf[mine] = qf[mine] + fold(dot(x_ref[...], v, TN))
    for x_copy in x_copies:
        x_copy.wait()
    qf[theirs] = qf[theirs] + fold(dot(xo_ref[...], v, TN))
    m = qw.shape[0]
    qw[...] = jnp.where(left_half(qw.shape), qf[0:m], qf[m : 2 * m]) * (1.0 / n_dp)

    m1, m2 = m // 2, m // 8
    m3 = m2 // n_z
    quarter = xx * 2 + mp
    a1 = core * m1
    a2 = a1 + quarter * m2
    a3 = a2 + zz * m3
    copy = send(qw.at[rows((1 - core) * m1, m1)], q1, core_mate)
    copy.wait()
    sum1 = qw[rows(a1, m1)] + q1[...]
    qw[rows(a1, m1)] = sum1
    qb[...] = sum1.astype(jnp.bfloat16)
    squad = (y_mate, x_mate, far_mate)
    quarters = ((xx * 2 + 1 - mp), ((1 - xx) * 2 + mp), ((1 - xx) * 2 + 1 - mp))
    copies = [send(qb.at[rows(quarters[d] * m2, m2)], q2.at[d], squad[d]) for d in range(3)]
    sum2 = qw[rows(a2, m2)]
    for d, copy in enumerate(copies):
        copy.wait()
        sum2 = sum2 + q2[d].astype(jnp.float32)
    qw[rows(a2, m2)] = sum2
    qc[...] = sum2.astype(jnp.bfloat16)
    copies = [
        send(qc.at[rows(lax.rem(zz + k, n_z) * m3, m3)], q3.at[k - 1], lane[k - 1]) for k in range(1, n_z)
    ]
    sum3 = qw[rows(a3, m3)]
    for k, copy in enumerate(copies):
        copy.wait()
        sum3 = sum3 + q3[k].astype(jnp.float32)
    qg_ref[rows(a3, m3)] = sum3.astype(jnp.bfloat16)
    for group, part in ((lane, rows(a3, m3)), (squad, rows(a2, m2)), ((core_mate,), rows(a1, m1))):
        copies = [send(qg_ref.at[part], qg_ref.at[part], mate) for mate in group]
        for copy in copies:
            copy.wait()

    @pl.when(mp == 0)
    def _():
        qown_ref[...] = qg_ref[0:own, :].astype(jnp.float32)[:, :rank]

    @pl.when(mp == 1)
    def _():
        qown_ref[0 : m - own, :] = qg_ref[own:m, :].astype(jnp.float32)[:, :rank]
        low = qg_ref[0 : features - m, :].astype(jnp.float32)
        qown_ref[m - own : own, :] = pltpu.roll(low, rank, 1)[:, :rank]


def residue_kernel(x_ref, xo_ref, g_ref, e_ref, pa_ref, pb_ref, qg_ref, out_ref, xs, qq):
    own = x_ref.shape[1]
    m = qg_ref.shape[0]
    features = e_ref.shape[1]

    @pl.when(pl.program_id(0) == 0)
    def _():
        @pl.when(lax.axis_index("mp") == 0)
        def _():
            xs[:, :own] = x_ref[...]
            xs[:, own:] = xo_ref[...]

        @pl.when(lax.axis_index("mp") == 1)
        def _():
            xs[:, :own] = xo_ref[...]
            xs[:, own:] = x_ref[...]

        qq[...] = jnp.concatenate([qg_ref[...], qg_ref[...]], axis=1)

    for p_ref, lo, hi in ((pa_ref, 0, m), (pb_ref, m, features)):
        merged = dot(g_ref[...], xs[:, lo:hi], TN) + e_ref[:, lo:hi].astype(jnp.float32)
        approx = dot(p_ref[...], qq[0 : hi - lo, :], NT)
        out_ref[:, lo:hi] = (merged - approx).astype(jnp.bfloat16)


def per_device(inputs, grad_out, error, q_prev):
    n_dp = lax.axis_size("dp")
    n_z = n_dp // 4
    tokens, own = inputs.shape
    out_rows, features = error.shape
    rank = q_prev.shape[1]
    width = 2 * rank
    m = -(-features // 256) * 128
    f32, bf16 = jnp.float32, jnp.bfloat16
    n = out_rows // 2
    vmem = pl.BlockSpec(memory_space=pltpu.VMEM)
    copies = 2 + 1 + 2 * (n_z + 1) + 1 + 2 * (n_z + 3)
    basis, q_own, pa, pb, qg, x_other = pl.pallas_call(
        functools.partial(exchange_kernel, n_dp),
        out_shape=(
            jax.ShapeDtypeStruct((out_rows, rank), f32),
            jax.ShapeDtypeStruct((own, rank), f32),
            jax.ShapeDtypeStruct((out_rows, 2 * width), bf16),
            jax.ShapeDtypeStruct((out_rows, 2 * width), bf16),
            jax.ShapeDtypeStruct((m, width), bf16),
            jax.ShapeDtypeStruct((tokens, own), bf16),
        ),
        in_specs=[vmem, vmem, pl.BlockSpec(memory_space=pl.ANY), vmem],
        out_specs=(vmem,) * 6,
        scratch_shapes=[
            pltpu.VMEM((out_rows, features), bf16),
            pltpu.VMEM((2, own, width), bf16),
            pltpu.VMEM((tokens // 2, width), f32),
            pltpu.VMEM((tokens // 2, width), f32),
            pltpu.VMEM((n, width), f32),
            pltpu.VMEM((n // 2, width), f32),
            pltpu.VMEM((n // 4, width), f32),
            pltpu.VMEM((n_z - 1, n // 4 // n_z, width), f32),
            pltpu.VMEM((n, width), f32),
            pltpu.VMEM((rank, width), f32),
            pltpu.VMEM((rank, width), f32),
            pltpu.VMEM((2 * m, width), f32),
            pltpu.VMEM((m, width), f32),
            pltpu.VMEM((m // 2, width), f32),
            pltpu.VMEM((m // 2, width), bf16),
            pltpu.VMEM((3, m // 8, width), bf16),
            pltpu.VMEM((m // 8, width), bf16),
            pltpu.VMEM((n_z - 1, m // 8 // n_z, width), bf16),
            pltpu.SemaphoreType.DMA,
            pltpu.SemaphoreType.DMA((PIECES,)),
            pltpu.SemaphoreType.DMA((PIECES,)),
            pltpu.SemaphoreType.DMA((copies,)),
            pltpu.SemaphoreType.DMA((copies,)),
        ],
        compiler_params=pltpu.CompilerParams(
            collective_id=0, has_side_effects=True, vmem_limit_bytes=60 * 1024 * 1024
        ),
        name="exchange",
    )(inputs, grad_out, error, jnp.concatenate([q_prev, q_prev], axis=1))

    tile = min(256, out_rows)
    whole = lambda shape: pl.BlockSpec(shape, lambda i: (0, 0), pipeline_mode=pl.Buffered(1))
    new_error = pl.pallas_call(
        residue_kernel,
        grid=(out_rows // tile,),
        out_shape=jax.ShapeDtypeStruct(error.shape, bf16),
        in_specs=[
            whole((tokens, own)),
            whole((tokens, own)),
            pl.BlockSpec((tokens, tile), lambda i: (0, i)),
            pl.BlockSpec((tile, features), lambda i: (i, 0)),
            pl.BlockSpec((tile, 2 * width), lambda i: (i, 0)),
            pl.BlockSpec((tile, 2 * width), lambda i: (i, 0)),
            whole((m, width)),
        ],
        out_specs=pl.BlockSpec((tile, features), lambda i: (i, 0)),
        scratch_shapes=[pltpu.VMEM((tokens, features), bf16), pltpu.VMEM((m, 2 * width), bf16)],
        compiler_params=pltpu.CompilerParams(vmem_limit_bytes=60 * 1024 * 1024),
        name="residue",
    )(inputs, x_other, grad_out, error, pa, pb, qg)
    return new_error, basis, q_own


def general_form(inputs, grad_out, error, q_prev):
    highest = lax.Precision.HIGHEST
    replicas = lax.axis_size("dp")
    shards = lax.axis_size("mp")
    own_rows = grad_out.shape[1]
    rank = q_prev.shape[1]
    q_full = lax.all_gather(q_prev, "mp", axis=0, tiled=True)
    prod = lax.dot_general(
        grad_out,
        lax.all_gather(inputs, "mp", axis=1, tiled=True),
        (((0,), (0,)), ((), ())),
        preferred_element_type=jnp.float32,
    )
    merged = prod + error.astype(jnp.float32)
    local_p = jnp.dot(merged, q_full, precision=highest)
    factor = lax.psum(local_p, "dp") / replicas
    gram = lax.psum(jnp.dot(factor.T, factor, precision=highest), "mp")
    ridge = 0.01 * jnp.trace(gram) / rank + 1e-06
    gram = gram + ridge * jnp.eye(rank, dtype=jnp.float32)
    lower = jnp.linalg.cholesky(gram)
    p_hat = jax.scipy.linalg.solve_triangular(lower, factor.T, lower=True).T
    q_term = lax.dot_general(merged, p_hat, (((0,), (0,)), ((), ())), precision=highest)
    q_part = lax.psum_scatter(
        q_term.astype(jnp.bfloat16), "mp", scatter_dimension=0, tiled=True
    ).astype(jnp.float32)
    q_own = lax.psum(q_part, "dp") / replicas
    q_whole = lax.all_gather(q_own.astype(jnp.bfloat16), "mp", axis=0, tiled=True).astype(
        q_own.dtype
    )
    approx = jnp.dot(p_hat, q_whole.T, precision=highest)
    new_error = (merged - approx).astype(jnp.bfloat16)
    scale = jnp.sqrt(jnp.float32(own_rows * shards))
    return (new_error, p_hat * scale, q_own)


def solution(mesh):
    paired = mesh.shape["mp"] == 2 and mesh.shape["dp"] % 4 == 0 and mesh.shape["dp"] > 4
    return jax.shard_map(
        per_device if paired else general_form,
        mesh=mesh,
        in_specs=(P("dp", "mp"), P("dp", "mp"), P(("dp", "mp"), None), P("mp", None)),
        out_specs=(P(("dp", "mp"), None), P("mp", None), P("mp", None)),
        check_vma=False,
    )
```

```python
import functools

import jax
import jax.numpy as jnp
from jax import lax
from jax.experimental import pallas as pl
from jax.experimental.pallas import tpu as pltpu
from jax.sharding import PartitionSpec as P

MESH = pl.DeviceIdType.MESH
PIECE = 64
NN = (((1,), (0,)), ((), ()))
NT = (((1,), (1,)), ((), ()))


def dot(a, b, dims=NN):
    return lax.dot_general(a, b, dims, preferred_element_type=jnp.float32)


def exact(a, b, dims=NN):
    return lax.dot_general(a, b, dims, precision=lax.Precision.HIGHEST, preferred_element_type=jnp.float32)


def split(value):
    head = value.astype(jnp.bfloat16)
    rest = (value - head.astype(jnp.float32)).astype(jnp.bfloat16)
    return jnp.concatenate([head, rest], axis=0)


def fold(terms):
    rank = terms.shape[0] // 2
    return terms[:rank] + terms[rank:]


def inverse_factor(gram):
    rank = gram.shape[0]
    row = lax.broadcasted_iota(jnp.int32, gram.shape, 0)
    diag = row == lax.broadcasted_iota(jnp.int32, gram.shape, 1)
    ridge = 0.01 * jnp.sum(jnp.where(diag, gram, 0.0), keepdims=True) / rank + 1e-06
    work = gram + jnp.where(diag, ridge, 0.0)
    inverse = jnp.where(diag, 1.0, 0.0)
    row1 = lax.broadcasted_iota(jnp.int32, (rank, 1), 0)
    for k in range(rank - 1):
        pivot_row = work[k : k + 1, :]
        factor = jnp.where(row1 > k, work[:, k : k + 1], 0.0) / pivot_row[:, k : k + 1]
        inverse = inverse - factor * inverse[k : k + 1, :]
        work = work - factor * pivot_row
    pivots = jnp.sum(jnp.where(diag, work, 0.0), axis=1, keepdims=True)
    return inverse * lax.rsqrt(pivots)


def exchange_kernel(
    n_dp, x_hbm, g_ref, e_hbm, q_ref,
    basis_ref, qown_ref, ph_ref, gt_ref, qg_ref, xf_hbm,
    e_ref, xf, qs, u_send, u_recv, v_send, v_recv, pw, p1, p2, p3, pg, gs, gr, qf, xt, q1, qb, q2, qc, q3,
    load_sem, x_ssem, x_rsem, ssem, rsem,
):
    dp, mp = lax.axis_index("dp"), lax.axis_index("mp")
    core, xx, zz = lax.rem(dp, 2), lax.rem(dp // 2, 2), dp // 4
    n_z = n_dp // 4
    rank, own = q_ref.shape
    features = e_ref.shape[1]

    def device(d_core, d_x, d_y, k):
        z = lax.rem(zz + k, n_z)
        c = 1 - core if d_core else core
        x = 1 - xx if d_x else xx
        return ((z * 2 + x) * 2 + c, 1 - mp if d_y else mp)

    core_mate, x_mate, y_mate, far_mate = device(1, 0, 0, 0), device(0, 1, 0, 0), device(0, 0, 1, 0), device(0, 1, 1, 0)
    lane = [device(0, 0, 0, k) for k in range(1, n_z)]

    x_base = pl.multiple_of(mp * own, PIECE)
    mine = pl.ds(x_base, own)
    load_x = pltpu.make_async_copy(x_hbm, xf.at[mine], load_sem.at[0])
    load_e = pltpu.make_async_copy(e_hbm, e_ref, load_sem.at[1])
    load_x.start()
    load_e.start()
    barrier = pltpu.get_barrier_semaphore()
    mates = [core_mate, x_mate, y_mate, far_mate] + lane
    for mate in mates:
        pl.semaphore_signal(barrier, inc=1, device_id=mate, device_id_type=MESH)

    used = [0]

    def send(src, dst, mate):
        index = used[0]
        used[0] += 1
        copy = pltpu.make_async_remote_copy(
            src_ref=src, dst_ref=dst, send_sem=ssem.at[index], recv_sem=rsem.at[index],
            device_id=mate, device_id_type=MESH,
        )
        copy.start()
        return copy

    pieces = own // PIECE
    flying = []

    def start_x(count):
        for j in range(len(flying), min(pieces, len(flying) + count)):
            part = pl.ds(pl.multiple_of(x_base + j * PIECE, PIECE), PIECE)
            copy = pltpu.make_async_remote_copy(
                src_ref=xf.at[part], dst_ref=xf.at[part], send_sem=x_ssem.at[j], recv_sem=x_rsem.at[j],
                device_id=y_mate, device_id_type=MESH,
            )
            copy.start()
            flying.append(copy)

    q_pair = split(q_ref[...])
    qs[mp] = q_pair
    pl.semaphore_wait(barrier, len(mates))
    my_half = pl.ds(pl.multiple_of(core * rank, 16), rank)
    q_copy = send(qs.at[mp, my_half], qs.at[mp, my_half], y_mate)
    load_x.wait()
    u_own = fold(dot(q_pair, xf[mine]))
    u_send[...] = u_own
    u_copy = send(u_send, u_recv, y_mate)
    gt_ref[...] = g_ref[...].T
    q_copy.wait()
    q_pass = send(qs.at[1 - mp, my_half], qs.at[1 - mp, my_half], core_mate)
    start_x(STEPS[0])
    u_copy.wait()
    p_part = dot(split(u_own + u_recv[...]), g_ref[...])
    load_e.wait()
    q_pass.wait()
    start_x(STEPS[1])
    q_all = jnp.concatenate([qs[0], qs[1]], axis=1)
    pw[...] = fold(p_part + dot(q_all, e_ref[...], NT))

    def part(offset, size):
        return pl.ds(pl.multiple_of(offset, size), size)

    n = pw.shape[1]
    n1, n2 = n // 2, n // 4
    height = rank // n_z
    b1 = part(core * n1, n1)
    b2 = part(core * n1 + xx * n2, n2)
    level = part(zz * height, height)
    levels = [part(lax.rem(zz + k, n_z) * height, height) for k in range(1, n_z)]
    copy = send(pw.at[:, part((1 - core) * n1, n1)], p1, core_mate)
    copy.wait()
    pw[:, b1] = pw[:, b1] + p1[...]
    copy = send(pw.at[:, part(core * n1 + (1 - xx) * n2, n2)], p2, x_mate)
    start_x(STEPS[2])
    copy.wait()
    pw[:, b2] = pw[:, b2] + p2[...]
    copies = [send(pw.at[levels[k], b2], p3.at[k], lane[k]) for k in range(n_z - 1)]
    start_x(STEPS[3])
    total = pw[level, b2]
    for k, copy in enumerate(copies):
        copy.wait()
        total = total + p3[k]
    pg[level, b2] = total * (1.0 / n_dp)
    copies = [send(pg.at[level, b2], pg.at[level, b2], mate) for mate in lane]
    start_x(STEPS[4])
    for copy in copies:
        copy.wait()
    copy = send(pg.at[:, b2], pg.at[:, b2], x_mate)
    start_x(STEPS[5])
    copy.wait()
    copy = send(pg.at[:, b1], pg.at[:, b1], core_mate)
    copy.wait()

    mean = pg[...]
    gs[...] = exact(mean, mean, NT)
    copy = send(gs, gr, y_mate)
    start_x(STEPS[6])
    copy.wait()
    p_hat = exact(inverse_factor(gs[...] + gr[...]), mean)
    basis_ref[...] = p_hat * jnp.sqrt(jnp.float32(n * lax.axis_size("mp")))
    p_pair = split(p_hat)
    v_own = fold(dot(p_pair, g_ref[...], NT))
    v_send[...] = v_own
    v_copy = send(v_send, v_recv, y_mate)
    start_x(STEPS[7])
    ph_ref[...] = p_pair.T

    m = qf.shape[1]
    qf[:, features:] = jnp.zeros((rank, m - features), jnp.float32)
    for lo in range(0, features, m // 4):
        hi = min(lo + m // 4, features)
        qf[:, lo:hi] = fold(dot(p_pair, e_ref[:, lo:hi]))
    v_copy.wait()
    xt[:, own:] = jnp.zeros((rank, xt.shape[1] - own), jnp.float32)
    xt[:, :own] = fold(dot(split(v_own + v_recv[...]), xf[mine], NT))
    m1, m2 = m // 2, m // 8

    @pl.when(mp == 0)
    def _():
        qf[:, :m1] = qf[:, :m1] + xt[...]

    @pl.when(mp == 1)
    def _():
        qf[:, features - m1 : features] = qf[:, features - m1 : features] + pltpu.roll(xt[...], m1 - own, 1)

    start_x(STEPS[8])
    a1 = part(core * m1, m1)
    a2 = part(core * m1 + (xx * 2 + mp) * m2, m2)
    copy = send(qf.at[:, part((1 - core) * m1, m1)], q1, core_mate)
    copy.wait()
    q1[...] = (qf[:, a1] + q1[...]) * (1.0 / n_dp)
    qb[...] = q1[...].astype(jnp.bfloat16)
    squad = (y_mate, x_mate, far_mate)
    quarters = ((xx * 2 + 1 - mp), ((1 - xx) * 2 + mp), ((1 - xx) * 2 + 1 - mp))
    copies = [send(qb.at[:, part(quarters[d] * m2, m2)], q2.at[d], squad[d]) for d in range(3)]
    start_x(STEPS[9])
    sum2 = q1[:, part((xx * 2 + mp) * m2, m2)]
    for d, copy in enumerate(copies):
        copy.wait()
        sum2 = sum2 + q2[d].astype(jnp.float32)
    p_sum = sum2.astype(jnp.bfloat16)
    qc[...] = p_sum
    copies = [send(qc.at[levels[k]], q3.at[k], lane[k]) for k in range(n_z - 1)]
    start_x(STEPS[10])
    qf[:, a2] = sum2
    sum3 = qf[level, a2]
    for k, copy in enumerate(copies):
        copy.wait()
        sum3 = sum3 + q3[k].astype(jnp.float32)
    qg_ref[level, a2] = sum3.astype(jnp.bfloat16)
    copies = [send(qg_ref.at[level, a2], qg_ref.at[level, a2], mate) for mate in lane]
    start_x(pieces)
    for copy in copies:
        copy.wait()
    copies = [send(qg_ref.at[:, a2], qg_ref.at[:, a2], mate) for mate in squad]
    for copy in flying:
        copy.wait()
    store_x = pltpu.make_async_copy(xf, xf_hbm, load_sem.at[2])
    store_x.start()
    for copy in copies:
        copy.wait()
    copy = send(qg_ref.at[:, a1], qg_ref.at[:, a1], core_mate)
    copy.wait()

    @pl.when(mp == 0)
    def _():
        qown_ref[...] = qg_ref[:, :own].astype(jnp.float32)

    @pl.when(mp == 1)
    def _():
        late = qg_ref[:, features - m1 : features].astype(jnp.float32)
        qown_ref[...] = pltpu.roll(late, own, 1)[:, :own]

    store_x.wait()


STEPS = (3, 3, 1, 2, 2, 1, 4, 3, 4, 1, 3)


def residue_kernel(gt_ref, x_ref, e_ref, ph_ref, qg_ref, out_ref):
    merged = dot(gt_ref[...], x_ref[...], NT) + e_ref[...].astype(jnp.float32)
    factor = qg_ref[...]
    approx = dot(ph_ref[...], jnp.concatenate([factor, factor], axis=0))
    out_ref[...] = (merged - approx).astype(jnp.bfloat16)


def per_device(inputs, grad_out, error, q_prev):
    n_dp = lax.axis_size("dp")
    n_z = n_dp // 4
    tokens, own = inputs.shape
    n, features = error.shape
    rank = q_prev.shape[1]
    m = -(-features // 1024) * 1024
    f32, bf16 = jnp.float32, jnp.bfloat16
    vmem, anywhere = pl.BlockSpec(memory_space=pltpu.VMEM), pl.BlockSpec(memory_space=pl.ANY)
    copies = 3 + 2 * (n_z + 1) + 2 + 2 * (n_z + 3)
    basis, q_own, ph, gt, qg, x_full = pl.pallas_call(
        functools.partial(exchange_kernel, n_dp),
        out_shape=(
            jax.ShapeDtypeStruct((rank, n), f32),
            jax.ShapeDtypeStruct((rank, own), f32),
            jax.ShapeDtypeStruct((n, 2 * rank), bf16),
            jax.ShapeDtypeStruct((n, tokens), bf16),
            jax.ShapeDtypeStruct((rank, m), bf16),
            jax.ShapeDtypeStruct((features, tokens), bf16),
        ),
        in_specs=[anywhere, vmem, anywhere, vmem],
        out_specs=(vmem,) * 5 + (anywhere,),
        scratch_shapes=[
            pltpu.VMEM((n, features), bf16),
            pltpu.VMEM((features, tokens), bf16),
            pltpu.VMEM((2, 2 * rank, own), bf16),
            pltpu.VMEM((rank, tokens), f32),
            pltpu.VMEM((rank, tokens), f32),
            pltpu.VMEM((rank, tokens), f32),
            pltpu.VMEM((rank, tokens), f32),
            pltpu.VMEM((rank, n), f32),
            pltpu.VMEM((rank, n // 2), f32),
            pltpu.VMEM((rank, n // 4), f32),
            pltpu.VMEM((n_z - 1, rank // n_z, n // 4), f32),
            pltpu.VMEM((rank, n), f32),
            pltpu.VMEM((rank, rank), f32),
            pltpu.VMEM((rank, rank), f32),
            pltpu.VMEM((rank, m), f32),
            pltpu.VMEM((rank, m // 2), f32),
            pltpu.VMEM((rank, m // 2), f32),
            pltpu.VMEM((rank, m // 2), bf16),
            pltpu.VMEM((3, rank, m // 8), bf16),
            pltpu.VMEM((rank, m // 8), bf16),
            pltpu.VMEM((n_z - 1, rank // n_z, m // 8), bf16),
            pltpu.SemaphoreType.DMA((3,)),
            pltpu.SemaphoreType.DMA((own // PIECE,)),
            pltpu.SemaphoreType.DMA((own // PIECE,)),
            pltpu.SemaphoreType.DMA((copies,)),
            pltpu.SemaphoreType.DMA((copies,)),
        ],
        compiler_params=pltpu.CompilerParams(
            collective_id=0, has_side_effects=True, vmem_limit_bytes=60 * 1024 * 1024
        ),
        name="exchange",
    )(inputs.T, grad_out, error, q_prev.T)

    tile = m // 8
    new_error = pl.pallas_call(
        residue_kernel,
        grid=(pl.cdiv(features, tile),),
        out_shape=jax.ShapeDtypeStruct(error.shape, bf16),
        in_specs=[
            pl.BlockSpec((n, tokens), lambda i: (0, 0), pipeline_mode=pl.Buffered(1)),
            pl.BlockSpec((tile, tokens), lambda i: (i, 0)),
            pl.BlockSpec((n, tile), lambda i: (0, i)),
            pl.BlockSpec((n, 2 * rank), lambda i: (0, 0), pipeline_mode=pl.Buffered(1)),
            pl.BlockSpec((rank, tile), lambda i: (0, i)),
        ],
        out_specs=pl.BlockSpec((n, tile), lambda i: (0, i)),
        compiler_params=pltpu.CompilerParams(vmem_limit_bytes=60 * 1024 * 1024),
        name="residue",
    )(gt, x_full, error, ph, qg)
    return new_error, basis.T, q_own.T


def general_form(inputs, grad_out, error, q_prev):
    highest = lax.Precision.HIGHEST
    replicas = lax.axis_size("dp")
    shards = lax.axis_size("mp")
    own_rows = grad_out.shape[1]
    rank = q_prev.shape[1]
    q_full = lax.all_gather(q_prev, "mp", axis=0, tiled=True)
    prod = lax.dot_general(
        grad_out,
        lax.all_gather(inputs, "mp", axis=1, tiled=True),
        (((0,), (0,)), ((), ())),
        preferred_element_type=jnp.float32,
    )
    merged = prod + error.astype(jnp.float32)
    local_p = jnp.dot(merged, q_full, precision=highest)
    factor = lax.psum(local_p, "dp") / replicas
    gram = lax.psum(jnp.dot(factor.T, factor, precision=highest), "mp")
    ridge = 0.01 * jnp.trace(gram) / rank + 1e-06
    gram = gram + ridge * jnp.eye(rank, dtype=jnp.float32)
    lower = jnp.linalg.cholesky(gram)
    p_hat = jax.scipy.linalg.solve_triangular(lower, factor.T, lower=True).T
    q_term = lax.dot_general(merged, p_hat, (((0,), (0,)), ((), ())), precision=highest)
    q_part = lax.psum_scatter(
        q_term.astype(jnp.bfloat16), "mp", scatter_dimension=0, tiled=True
    ).astype(jnp.float32)
    q_own = lax.psum(q_part, "dp") / replicas
    q_whole = lax.all_gather(q_own.astype(jnp.bfloat16), "mp", axis=0, tiled=True).astype(
        q_own.dtype
    )
    approx = jnp.dot(p_hat, q_whole.T, precision=highest)
    new_error = (merged - approx).astype(jnp.bfloat16)
    scale = jnp.sqrt(jnp.float32(own_rows * shards))
    return (new_error, p_hat * scale, q_own)


def solution(mesh):
    paired = mesh.shape["mp"] == 2 and mesh.shape["dp"] % 4 == 0 and mesh.shape["dp"] > 4
    return jax.shard_map(
        per_device if paired else general_form,
        mesh=mesh,
        in_specs=(P("dp", "mp"), P("dp", "mp"), P(("dp", "mp"), None), P("mp", None)),
        out_specs=(P(("dp", "mp"), None), P("mp", None), P("mp", None)),
        check_vma=False,
    )
```

```python
import functools

import jax
import jax.numpy as jnp
from jax import lax
from jax.experimental import pallas as pl
from jax.experimental.pallas import tpu as pltpu
from jax.sharding import PartitionSpec as P

MESH = pl.DeviceIdType.MESH
PIECE = 64
NN = (((1,), (0,)), ((), ()))
NT = (((1,), (1,)), ((), ()))


def dot(a, b, dims=NN):
    return lax.dot_general(a, b, dims, preferred_element_type=jnp.float32)


def exact(a, b, dims=NN):
    return lax.dot_general(a, b, dims, precision=lax.Precision.HIGHEST, preferred_element_type=jnp.float32)


def split(value):
    head = value.astype(jnp.bfloat16)
    rest = (value - head.astype(jnp.float32)).astype(jnp.bfloat16)
    return jnp.concatenate([head, rest], axis=0)


def fold(terms):
    rank = terms.shape[0] // 2
    return terms[:rank] + terms[rank:]


def inverse_factor(gram):
    rank = gram.shape[0]
    row = lax.broadcasted_iota(jnp.int32, gram.shape, 0)
    diag = row == lax.broadcasted_iota(jnp.int32, gram.shape, 1)
    ridge = 0.01 * jnp.sum(jnp.where(diag, gram, 0.0), keepdims=True) / rank + 1e-06
    work = gram + jnp.where(diag, ridge, 0.0)
    inverse = jnp.where(diag, 1.0, 0.0)
    row1 = lax.broadcasted_iota(jnp.int32, (rank, 1), 0)
    for k in range(0, rank, 2):
        first, second = work[k : k + 1, :], work[k + 1 : k + 2, :]
        one, two = work[:, k : k + 1], work[:, k + 1 : k + 2]
        cross = first[:, k + 1 : k + 2]
        ratio = second[:, k : k + 1] / first[:, k : k + 1]
        factor = jnp.where(row1 > k, one, 0.0) / first[:, k : k + 1]
        pivot = second[:, k + 1 : k + 2] - ratio * cross
        later = jnp.where(row1 > k + 1, two - factor * cross, 0.0) / pivot
        second = second - ratio * first
        begin = inverse[k : k + 1, :]
        follow = inverse[k + 1 : k + 2, :] - ratio * begin
        inverse = inverse - factor * begin - later * follow
        work = work - factor * first - later * second
    pivots = jnp.sum(jnp.where(diag, work, 0.0), axis=1, keepdims=True)
    return inverse * lax.rsqrt(pivots)


def exchange_kernel(
    n_dp, x_hbm, g_ref, e_hbm, q_ref,
    basis_ref, qown_ref, ph_ref, gt_ref, qg_ref, xf_hbm,
    e_ref, xf, qs, u_send, u_recv, v_send, v_recv, pw, p1, p2, p3, pg, gs, gr, qf, xt, q1, qb, q2, qc, q3,
    load_sem, x_ssem, x_rsem, ssem, rsem,
):
    dp, mp = lax.axis_index("dp"), lax.axis_index("mp")
    core, xx, zz = lax.rem(dp, 2), lax.rem(dp // 2, 2), dp // 4
    n_z = n_dp // 4
    rank, own = q_ref.shape
    features = e_ref.shape[1]

    def device(d_core, d_x, d_y, k):
        z = lax.rem(zz + k, n_z)
        c = 1 - core if d_core else core
        x = 1 - xx if d_x else xx
        return ((z * 2 + x) * 2 + c, 1 - mp if d_y else mp)

    core_mate, x_mate, y_mate, far_mate = device(1, 0, 0, 0), device(0, 1, 0, 0), device(0, 0, 1, 0), device(0, 1, 1, 0)
    lane = [device(0, 0, 0, k) for k in range(1, n_z)]

    x_base = pl.multiple_of(mp * own, PIECE)
    mine = pl.ds(x_base, own)
    load_x = pltpu.make_async_copy(x_hbm, xf.at[mine], load_sem.at[0])
    load_e = pltpu.make_async_copy(e_hbm, e_ref, load_sem.at[1])
    load_x.start()
    load_e.start()
    barrier = pltpu.get_barrier_semaphore()
    mates = [core_mate, x_mate, y_mate, far_mate] + lane
    for mate in mates:
        pl.semaphore_signal(barrier, inc=1, device_id=mate, device_id_type=MESH)

    used = [0]

    def send(src, dst, mate):
        index = used[0]
        used[0] += 1
        copy = pltpu.make_async_remote_copy(
            src_ref=src, dst_ref=dst, send_sem=ssem.at[index], recv_sem=rsem.at[index],
            device_id=mate, device_id_type=MESH,
        )
        copy.start()
        return copy

    pieces = own // PIECE
    flying = []

    def start_x(count):
        for j in range(len(flying), min(pieces, len(flying) + count)):
            part = pl.ds(pl.multiple_of(x_base + j * PIECE, PIECE), PIECE)
            copy = pltpu.make_async_remote_copy(
                src_ref=xf.at[part], dst_ref=xf.at[part], send_sem=x_ssem.at[j], recv_sem=x_rsem.at[j],
                device_id=y_mate, device_id_type=MESH,
            )
            copy.start()
            flying.append(copy)

    q_pair = split(q_ref[...])
    qs[mp] = q_pair
    pl.semaphore_wait(barrier, len(mates))
    my_half = pl.ds(pl.multiple_of(core * rank, 16), rank)
    q_copy = send(qs.at[mp, my_half], qs.at[mp, my_half], y_mate)
    load_x.wait()
    u_own = fold(dot(q_pair, xf[mine]))
    u_send[...] = u_own
    u_copy = send(u_send, u_recv, y_mate)
    gt_ref[...] = g_ref[...].T
    q_copy.wait()
    q_pass = send(qs.at[1 - mp, my_half], qs.at[1 - mp, my_half], core_mate)
    start_x(STEPS[0])
    u_copy.wait()
    p_part = dot(split(u_own + u_recv[...]), g_ref[...])
    load_e.wait()
    q_pass.wait()
    start_x(STEPS[1])
    q_all = jnp.concatenate([qs[0], qs[1]], axis=1)
    pw[...] = fold(p_part + dot(q_all, e_ref[...], NT))

    def part(offset, size):
        return pl.ds(pl.multiple_of(offset, size), size)

    n = pw.shape[1]
    n1, n2 = n // 2, n // 4
    height = rank // n_z
    b1 = part(core * n1, n1)
    b2 = part(core * n1 + xx * n2, n2)
    level = part(zz * height, height)
    levels = [part(lax.rem(zz + k, n_z) * height, height) for k in range(1, n_z)]
    copy = send(pw.at[:, part((1 - core) * n1, n1)], p1, core_mate)
    copy.wait()
    pw[:, b1] = pw[:, b1] + p1[...]
    copy = send(pw.at[:, part(core * n1 + (1 - xx) * n2, n2)], p2, x_mate)
    start_x(STEPS[2])
    copy.wait()
    pw[:, b2] = pw[:, b2] + p2[...]
    copies = [send(pw.at[levels[k], b2], p3.at[k], lane[k]) for k in range(n_z - 1)]
    start_x(STEPS[3])
    total = pw[level, b2]
    for k, copy in enumerate(copies):
        copy.wait()
        total = total + p3[k]
    pg[level, b2] = total * (1.0 / n_dp)
    copies = [send(pg.at[level, b2], pg.at[level, b2], mate) for mate in lane]
    start_x(STEPS[4])
    for copy in copies:
        copy.wait()
    copy = send(pg.at[:, b2], pg.at[:, b2], x_mate)
    start_x(STEPS[5])
    copy.wait()
    copy = send(pg.at[:, b1], pg.at[:, b1], core_mate)
    copy.wait()

    mean = pg[...]
    gs[...] = exact(mean, mean, NT)
    copy = send(gs, gr, y_mate)
    start_x(STEPS[6])
    copy.wait()
    p_hat = exact(inverse_factor(gs[...] + gr[...]), mean)
    basis_ref[...] = p_hat * jnp.sqrt(jnp.float32(n * lax.axis_size("mp")))
    p_pair = split(p_hat)
    v_own = fold(dot(p_pair, g_ref[...], NT))
    v_send[...] = v_own
    v_copy = send(v_send, v_recv, y_mate)
    start_x(STEPS[7])
    ph_ref[...] = p_pair.T

    m = qf.shape[1]
    qf[:, features:] = jnp.zeros((rank, m - features), jnp.float32)
    for lo in range(0, features, m // 4):
        hi = min(lo + m // 4, features)
        qf[:, lo:hi] = fold(dot(p_pair, e_ref[:, lo:hi]))
    v_copy.wait()
    xt[:, own:] = jnp.zeros((rank, xt.shape[1] - own), jnp.float32)
    xt[:, :own] = fold(dot(split(v_own + v_recv[...]), xf[mine], NT))
    m1, m2 = m // 2, m // 8

    @pl.when(mp == 0)
    def _():
        qf[:, :m1] = qf[:, :m1] + xt[...]

    @pl.when(mp == 1)
    def _():
        qf[:, features - m1 : features] = qf[:, features - m1 : features] + pltpu.roll(xt[...], m1 - own, 1)

    start_x(STEPS[8])
    a1 = part(core * m1, m1)
    a2 = part(core * m1 + (xx * 2 + mp) * m2, m2)
    copy = send(qf.at[:, part((1 - core) * m1, m1)], q1, core_mate)
    copy.wait()
    q1[...] = (qf[:, a1] + q1[...]) * (1.0 / n_dp)
    qb[...] = q1[...].astype(jnp.bfloat16)
    squad = (y_mate, x_mate, far_mate)
    quarters = ((xx * 2 + 1 - mp), ((1 - xx) * 2 + mp), ((1 - xx) * 2 + 1 - mp))
    copies = [send(qb.at[:, part(quarters[d] * m2, m2)], q2.at[d], squad[d]) for d in range(3)]
    start_x(STEPS[9])
    sum2 = q1[:, part((xx * 2 + mp) * m2, m2)]
    for d, copy in enumerate(copies):
        copy.wait()
        sum2 = sum2 + q2[d].astype(jnp.float32)
    p_sum = sum2.astype(jnp.bfloat16)
    qc[...] = p_sum
    copies = [send(qc.at[levels[k]], q3.at[k], lane[k]) for k in range(n_z - 1)]
    start_x(STEPS[10])
    qf[:, a2] = sum2
    sum3 = qf[level, a2]
    for k, copy in enumerate(copies):
        copy.wait()
        sum3 = sum3 + q3[k].astype(jnp.float32)
    qg_ref[level, a2] = sum3.astype(jnp.bfloat16)
    copies = [send(qg_ref.at[level, a2], qg_ref.at[level, a2], mate) for mate in lane]
    start_x(pieces)
    for copy in copies:
        copy.wait()
    copies = [send(qg_ref.at[:, a2], qg_ref.at[:, a2], mate) for mate in squad]
    for copy in flying:
        copy.wait()
    store_x = pltpu.make_async_copy(xf, xf_hbm, load_sem.at[2])
    store_x.start()
    for copy in copies:
        copy.wait()
    copy = send(qg_ref.at[:, a1], qg_ref.at[:, a1], core_mate)
    copy.wait()

    @pl.when(mp == 0)
    def _():
        qown_ref[...] = qg_ref[:, :own].astype(jnp.float32)

    @pl.when(mp == 1)
    def _():
        late = qg_ref[:, features - m1 : features].astype(jnp.float32)
        qown_ref[...] = pltpu.roll(late, own, 1)[:, :own]

    store_x.wait()


STEPS = (3, 4, 2, 3, 3, 1, 4, 4, 1, 0, 4)


def residue_kernel(gt_ref, x_ref, e_ref, ph_ref, qg_ref, out_ref):
    merged = dot(gt_ref[...], x_ref[...], NT) + e_ref[...].astype(jnp.float32)
    factor = qg_ref[...]
    approx = dot(ph_ref[...], jnp.concatenate([factor, factor], axis=0))
    out_ref[...] = (merged - approx).astype(jnp.bfloat16)


def per_device(inputs, grad_out, error, q_prev):
    n_dp = lax.axis_size("dp")
    n_z = n_dp // 4
    tokens, own = inputs.shape
    n, features = error.shape
    rank = q_prev.shape[1]
    m = -(-features // 1024) * 1024
    f32, bf16 = jnp.float32, jnp.bfloat16
    vmem, anywhere = pl.BlockSpec(memory_space=pltpu.VMEM), pl.BlockSpec(memory_space=pl.ANY)
    copies = 3 + 2 * (n_z + 1) + 2 + 2 * (n_z + 3)
    basis, q_own, ph, gt, qg, x_full = pl.pallas_call(
        functools.partial(exchange_kernel, n_dp),
        out_shape=(
            jax.ShapeDtypeStruct((rank, n), f32),
            jax.ShapeDtypeStruct((rank, own), f32),
            jax.ShapeDtypeStruct((n, 2 * rank), bf16),
            jax.ShapeDtypeStruct((n, tokens), bf16),
            jax.ShapeDtypeStruct((rank, m), bf16),
            jax.ShapeDtypeStruct((features, tokens), bf16),
        ),
        in_specs=[anywhere, vmem, anywhere, vmem],
        out_specs=(vmem,) * 5 + (anywhere,),
        scratch_shapes=[
            pltpu.VMEM((n, features), bf16),
            pltpu.VMEM((features, tokens), bf16),
            pltpu.VMEM((2, 2 * rank, own), bf16),
            pltpu.VMEM((rank, tokens), f32),
            pltpu.VMEM((rank, tokens), f32),
            pltpu.VMEM((rank, tokens), f32),
            pltpu.VMEM((rank, tokens), f32),
            pltpu.VMEM((rank, n), f32),
            pltpu.VMEM((rank, n // 2), f32),
            pltpu.VMEM((rank, n // 4), f32),
            pltpu.VMEM((n_z - 1, rank // n_z, n // 4), f32),
            pltpu.VMEM((rank, n), f32),
            pltpu.VMEM((rank, rank), f32),
            pltpu.VMEM((rank, rank), f32),
            pltpu.VMEM((rank, m), f32),
            pltpu.VMEM((rank, m // 2), f32),
            pltpu.VMEM((rank, m // 2), f32),
            pltpu.VMEM((rank, m // 2), bf16),
            pltpu.VMEM((3, rank, m // 8), bf16),
            pltpu.VMEM((rank, m // 8), bf16),
            pltpu.VMEM((n_z - 1, rank // n_z, m // 8), bf16),
            pltpu.SemaphoreType.DMA((3,)),
            pltpu.SemaphoreType.DMA((own // PIECE,)),
            pltpu.SemaphoreType.DMA((own // PIECE,)),
            pltpu.SemaphoreType.DMA((copies,)),
            pltpu.SemaphoreType.DMA((copies,)),
        ],
        compiler_params=pltpu.CompilerParams(
            collective_id=0, has_side_effects=True, vmem_limit_bytes=60 * 1024 * 1024
        ),
        name="exchange",
    )(inputs.T, grad_out, error, q_prev.T)

    tile = m // 4
    new_error = pl.pallas_call(
        residue_kernel,
        grid=(pl.cdiv(features, tile),),
        out_shape=jax.ShapeDtypeStruct(error.shape, bf16),
        in_specs=[
            pl.BlockSpec((n, tokens), lambda i: (0, 0), pipeline_mode=pl.Buffered(1)),
            pl.BlockSpec((tile, tokens), lambda i: (i, 0)),
            pl.BlockSpec((n, tile), lambda i: (0, i)),
            pl.BlockSpec((n, 2 * rank), lambda i: (0, 0), pipeline_mode=pl.Buffered(1)),
            pl.BlockSpec((rank, tile), lambda i: (0, i)),
        ],
        out_specs=pl.BlockSpec((n, tile), lambda i: (0, i)),
        compiler_params=pltpu.CompilerParams(vmem_limit_bytes=60 * 1024 * 1024),
        name="residue",
    )(gt, x_full, error, ph, qg)
    return new_error, basis.T, q_own.T


def general_form(inputs, grad_out, error, q_prev):
    highest = lax.Precision.HIGHEST
    replicas = lax.axis_size("dp")
    shards = lax.axis_size("mp")
    own_rows = grad_out.shape[1]
    rank = q_prev.shape[1]
    q_full = lax.all_gather(q_prev, "mp", axis=0, tiled=True)
    prod = lax.dot_general(
        grad_out,
        lax.all_gather(inputs, "mp", axis=1, tiled=True),
        (((0,), (0,)), ((), ())),
        preferred_element_type=jnp.float32,
    )
    merged = prod + error.astype(jnp.float32)
    local_p = jnp.dot(merged, q_full, precision=highest)
    factor = lax.psum(local_p, "dp") / replicas
    gram = lax.psum(jnp.dot(factor.T, factor, precision=highest), "mp")
    ridge = 0.01 * jnp.trace(gram) / rank + 1e-06
    gram = gram + ridge * jnp.eye(rank, dtype=jnp.float32)
    lower = jnp.linalg.cholesky(gram)
    p_hat = jax.scipy.linalg.solve_triangular(lower, factor.T, lower=True).T
    q_term = lax.dot_general(merged, p_hat, (((0,), (0,)), ((), ())), precision=highest)
    q_part = lax.psum_scatter(
        q_term.astype(jnp.bfloat16), "mp", scatter_dimension=0, tiled=True
    ).astype(jnp.float32)
    q_own = lax.psum(q_part, "dp") / replicas
    q_whole = lax.all_gather(q_own.astype(jnp.bfloat16), "mp", axis=0, tiled=True).astype(
        q_own.dtype
    )
    approx = jnp.dot(p_hat, q_whole.T, precision=highest)
    new_error = (merged - approx).astype(jnp.bfloat16)
    scale = jnp.sqrt(jnp.float32(own_rows * shards))
    return (new_error, p_hat * scale, q_own)


def solution(mesh):
    paired = mesh.shape["mp"] == 2 and mesh.shape["dp"] % 4 == 0 and mesh.shape["dp"] > 4
    return jax.shard_map(
        per_device if paired else general_form,
        mesh=mesh,
        in_specs=(P("dp", "mp"), P("dp", "mp"), P(("dp", "mp"), None), P("mp", None)),
        out_specs=(P(("dp", "mp"), None), P("mp", None), P("mp", None)),
        check_vma=False,
    )
```
